32 devices in a mesh: expert: 4 (over x, core), dp: 8 (over z, y).
Axes of the slice: x: 2, y: 2, z: 4, core: 2. Of those that a mesh axis runs over, the one named last changes fastest.
Arguments:
- layer_input: bfloat16 [8192, 768], P(('expert', 'dp')), may hold values from -6 to 6
- routes: int32 [8192, 2], P(('expert', 'dp')), may hold values from 0 to 15, all different within a row
- priority: int32 [32, 512], P(('expert', 'dp')), may hold values from 0 to 511, each once within a row
- cont_ids: int32 [32, 128], P(('expert', 'dp')), may hold values from 0 to 3, never falling along the last dimension, each value on 1 to 64 neighbouring positions
- cotangent: bfloat16 [8192, 768], P(('expert', 'dp')), may hold values from -6 to 6
- norm1_gain: bfloat16 [768], P('dp'), may hold values from 0.099609375 to 1.8984375
- qkv_weight: bfloat16 [768, 2304], P('dp'), may hold values from -0.21875 to 0.21875
- out_weight: bfloat16 [768, 768], P('dp'), may hold values from -0.875 to 0.875
- norm2_gain: bfloat16 [768], P('dp'), may hold values from 0.099609375 to 1.8984375
- router_weight: bfloat16 [768, 16], P('dp'), may hold values from -0.109375 to 0.109375
- shared_in: bfloat16 [768, 4096], P('dp'), may hold values from -0.21875 to 0.21875
- shared_out: bfloat16 [2048, 768], P('dp'), may hold values from -0.125 to 0.125
- expert_in: bfloat16 [16, 768, 4096], P('expert', 'dp'), may hold values from -0.21875 to 0.21875
- expert_out: bfloat16 [16, 2048, 768], P('expert', 'dp'), may hold values from -0.1875 to 0.1875
Outputs:
- layer_output: bfloat16 [8192, 768], P(('expert', 'dp'))
- input_grad: float32 [8192, 768], P(('expert', 'dp'))
- norm1_grad: float32 [768], P('dp')
- qkv_grad: float32 [768, 2304], P('dp')
- out_weight_grad: float32 [768, 768], P('dp')
- norm2_grad: float32 [768], P('dp')
- router_grad: float32 [768, 16], P('dp')
- shared_in_grad: float32 [768, 4096], P('dp')
- shared_out_grad: float32 [2048, 768], P('dp')
- expert_in_grad: float32 [16, 768, 4096], P('expert', 'dp')
- expert_out_grad: float32 [16, 2048, 768], P('expert', 'dp')
The draws below stay inside these ranges and needn't reach their ends.
Inputs may be any that keep to these rules, and one draw needn't show every extreme that they name: `routes`: each token names 2 different experts. `priority`: each row is a permutation of the 512 pairs of its group. `cont_ids`: each row never falls; each of the 4 continuations has 1 to 64 tokens, one exactly 64.
All inputs are finite; a program needn't handle non-finite values.
Results may differ from the reference program's by a relative error of at most 0.02.
Values may be sent and summed in bfloat16 or wider, within the bound.
No kernel may reach another device: no remote copies, remote signals or barrier semaphores. Data moves between devices by JAX's collectives and lax.ppermute only.
A program may use at most 192 MiB of HBM per device.

```python
import math
import jax
import jax.numpy as jnp
import numpy as np
from jax import lax

D = 768
HEADS = 12
HEAD = 64
EXPERTS = 16
FF = 2048
TOP = 2
FS = 2048
CONTS = 4
TOK_DEV = 256
PROMPT = 128
CONT_MOST = 64
CAP = 40
GROUPS = 32
TOKENS = 8192


def steps_of(rng, dims, cuts, least, largest):
    loudness = 1.0
    for axis_at, shards_of in cuts:
        draws = jax.random.uniform(jax.random.fold_in(jax.random.fold_in(rng, 6), axis_at), (shards_of,), jnp.float32, least / len(cuts), largest / len(cuts))
        loudness = loudness * jnp.repeat(jnp.exp(draws), dims[axis_at] // shards_of).reshape((-1,) + (1,) * (len(dims) - 1 - axis_at))
    return loudness


def picks_of(own_key, rows, number_of, top, lift):
    order = jax.random.permutation(jax.random.fold_in(own_key, 1), number_of)
    favour = order
    for power in range(3):
        favour = favour * favour // number_of
    favour = favour * lift // number_of
    lots = jax.random.randint(jax.random.fold_in(own_key, 2), (rows, number_of), 0, 4096) + favour
    fixed_rows = jax.random.permutation(jax.random.fold_in(own_key, 3), rows)[jnp.arange(number_of) % rows]
    lots = jnp.where(jnp.arange(rows)[:, None] == fixed_rows[None, :], 1 << 14, lots)
    score = lots * number_of + jnp.arange(number_of)
    return lax.top_k(score.astype(jnp.int32), top)[1].astype(jnp.int32)


def split_up(amount, total, bound, slope):
    loads = [(1 << 20) // math.isqrt(grade ** slope) + 1 for grade in range(2, amount + 1)]
    surplus, holding = total - bound - (amount - 1), [1] * (amount - 1)
    while surplus > 0:
        free = [i for i in range(amount - 1) if holding[i] < bound]
        whole, remaining = sum([loads[i] for i in free]), surplus
        for i in free:
            more = min(bound - holding[i], max(1, remaining * loads[i] // whole), surplus)
            holding[i] = holding[i] + more
            surplus = surplus - more
    return np.array([bound] + holding)


def uneven_parts(key, amount, total, limit, lean):
    if amount == 2:
        one = jax.random.randint(key, (), max(1, total - limit), min(limit, total - 1) + 1)
        return jnp.stack([one, total - one])
    tallies = jnp.asarray(split_up(amount, total, limit, lean), jnp.int32)
    twos = (amount - 1) // 2
    source_of, receiver = tallies[1:1 + 2 * twos:2], tallies[2:2 + 2 * twos:2]
    room = jnp.minimum(source_of - 1, limit - receiver)
    passed = jax.random.randint(jax.random.fold_in(key, 1), (twos,), 0, 1 << 20) % (room + 1)
    tallies = tallies.at[1:1 + 2 * twos:2].set(source_of - passed).at[2:2 + 2 * twos:2].set(receiver + passed)
    return tallies[jax.random.permutation(jax.random.fold_in(key, 2), amount)]


def scatter_about(stream_key, extent, scale, bound, cuts=(), held_as=jnp.bfloat16):
    drawn = scale * jax.random.normal(stream_key, extent, jnp.float32)
    if cuts:
        drawn = drawn * steps_of(stream_key, extent, cuts, -0.22, 0.18)
    return jnp.clip(drawn, -bound, bound).astype(held_as)


def setup_inputs(seed: int = 0) -> dict:
    seeds = jax.random.split(jax.random.key(seed), 15)
    layer_input = scatter_about(seeds[0], (TOKENS, D), 1.0, 6.0, ((0, 32),))
    routes = picks_of(seeds[1], TOKENS, EXPERTS, TOP, 1024)
    priority = jax.vmap(lambda own: jax.random.permutation(own, TOK_DEV * TOP))(jax.random.split(seeds[2], GROUPS)).reshape((GROUPS, TOK_DEV * TOP)).astype(jnp.int32)
    cont_ids = jax.vmap(lambda own: jnp.searchsorted(jnp.cumsum(uneven_parts(own, CONTS, TOK_DEV - PROMPT, CONT_MOST, 1)), jnp.arange(TOK_DEV - PROMPT), side="right"))(jax.random.split(seeds[3], GROUPS)).reshape((GROUPS, TOK_DEV - PROMPT)).astype(jnp.int32)
    cotangent = scatter_about(seeds[4], (TOKENS, D), 1.0, 6.0, ((0, 32),))
    norm1_gain = jnp.clip(1.0 + 0.18 * jax.random.normal(seeds[5], (D,), jnp.float32), 0.099609375, 1.8984375).astype(jnp.bfloat16)
    qkv_weight = scatter_about(seeds[6], (D, 3 * D), D ** -0.5, 0.21875, ((0, 8),))
    out_weight = scatter_about(seeds[7], (D, D), (D // 16) ** -0.5, 0.875, ((0, 8),))
    norm2_gain = jnp.clip(1.0 + 0.18 * jax.random.normal(seeds[8], (D,), jnp.float32), 0.099609375, 1.8984375).astype(jnp.bfloat16)
    router_weight = scatter_about(seeds[9], (D, EXPERTS), (4 * D) ** -0.5, 0.109375, ((0, 8),))
    shared_in = scatter_about(seeds[10], (D, 2 * FS), D ** -0.5, 0.21875, ((0, 8),))
    shared_out = scatter_about(seeds[11], (FS, D), FS ** -0.5, 0.125, ((0, 8),))
    expert_in = scatter_about(seeds[12], (EXPERTS, D, 2 * FF), D ** -0.5, 0.21875, ((0, 4), (1, 8)))
    expert_out = scatter_about(seeds[13], (EXPERTS, FF, D), (FF // 2) ** -0.5, 0.1875, ((0, 4), (1, 8)))
    return {"layer_input": layer_input, "routes": routes, "priority": priority, "cont_ids": cont_ids, "cotangent": cotangent, "norm1_gain": norm1_gain, "qkv_weight": qkv_weight, "out_weight": out_weight, "norm2_gain": norm2_gain, "router_weight": router_weight, "shared_in": shared_in, "shared_out": shared_out, "expert_in": expert_in, "expert_out": expert_out}


@jax.custom_vjp
def low(v):
    return lax.optimization_barrier(v.astype(jnp.bfloat16)).astype(jnp.float32)

@jax.custom_vjp
def low_back(v):
    return v

def low_keep(v):
    return (low(v), None)

def low_pass(kept, grad):
    return (grad,)

def back_keep(v):
    return (v, None)

def back_low(kept, grad):
    return (low(grad),)
low.defvjp(low_keep, low_pass)
low_back.defvjp(back_keep, back_low)
epsilon = 1e-06
rope_base = 10000.0
highest = lax.Precision.HIGHEST

def matmul(left_side, right_side):
    return jnp.dot(left_side, right_side, precision=highest)

def rms_scale(values, gain_vector):
    return values * lax.rsqrt(lax.optimization_barrier(jnp.mean(values * values, axis=-1, keepdims=True)) + epsilon) * gain_vector

def layout(cont_row):
    labels = jnp.arange(CONTS, dtype=jnp.int32)
    member = cont_row[:, None] == labels[None, :]
    lengths = lax.optimization_barrier(jnp.sum(member.astype(jnp.int32), axis=0))
    starts = jnp.cumsum(lengths) - lengths
    begins = lax.optimization_barrier(jnp.sum(jnp.where(member, starts[None, :], 0), axis=1))
    offsets = jnp.arange(cont_row.shape[0], dtype=jnp.int32) - begins
    position = jnp.concatenate([jnp.arange(PROMPT, dtype=jnp.int32), PROMPT + offsets])
    segment = jnp.concatenate([jnp.full((PROMPT,), -1, jnp.int32), cont_row])
    rows_at = jnp.arange(TOK_DEV, dtype=jnp.int32)
    visible = (rows_at[None, :] <= rows_at[:, None]) & (segment[None, :] == segment[:, None]) | (rows_at[None, :] < PROMPT) & (rows_at[:, None] >= PROMPT)
    half_dim = HEAD // 2
    frequency = rope_base ** (-(jnp.arange(half_dim, dtype=jnp.float32) * 2.0) / HEAD)
    angles = position.astype(jnp.float32)[:, None] * frequency[None, :]
    cosine = jnp.concatenate([jnp.cos(angles), jnp.cos(angles)], axis=1)
    sine_table = jnp.concatenate([jnp.sin(angles), jnp.sin(angles)], axis=1)
    return (visible, cosine, sine_table)

def rotate(values, cosine, sine_table):
    half_dim = HEAD // 2
    turned = jnp.concatenate([-values[..., half_dim:], values[..., :half_dim]], axis=-1)
    return values * cosine[:, None, :] + turned * sine_table[:, None, :]

def slot_plan(route_rows, prio_row):
    pair_expert = route_rows.reshape(-1)
    onehot = (pair_expert[:, None] == jnp.arange(EXPERTS, dtype=jnp.int32)[None, :]).astype(jnp.int32)
    ordered = jnp.zeros_like(onehot).at[prio_row].set(onehot)
    before = jnp.cumsum(ordered, axis=0) - ordered
    slot_index = lax.optimization_barrier(jnp.sum(before[prio_row] * onehot, axis=1))
    return (pair_expert, slot_index)

def group_forward(params, tokens, route_rows, prio_row, cont_row):
    gain_one, qkv_weight, out_weight, gain_two, router_weight, shared_in, shared_out, expert_in, expert_out = params
    visible, cosine, sine_table = layout(cont_row)
    row_count = tokens.shape[0]
    normed_one = low(rms_scale(tokens, gain_one))
    projected = low_back(matmul(normed_one, qkv_weight))
    queries = low(rotate(projected[:, :D].reshape(row_count, HEADS, HEAD), cosine, sine_table))
    key_heads = low(rotate(projected[:, D:2 * D].reshape(row_count, HEADS, HEAD), cosine, sine_table))
    values = low(projected[:, 2 * D:].reshape(row_count, HEADS, HEAD))
    scores = low_back(jnp.einsum('qhd,khd->hqk', queries, key_heads, precision=highest) * 0.125)
    scores = jnp.where(visible[None], scores, -1e+30)
    attention = low(jax.nn.softmax(scores, axis=-1))
    context = low(low_back(jnp.einsum('hqk,khd->qhd', attention, values, precision=highest))).reshape(row_count, D)
    residual = tokens + low_back(matmul(context, out_weight))
    normed_two = low(rms_scale(residual, gain_two))
    gate_probs = jax.nn.softmax(matmul(normed_two, router_weight), axis=-1)
    shared_pre = low_back(matmul(normed_two, shared_in))
    shared_hidden = low(jax.nn.silu(shared_pre[:, :FS]) * shared_pre[:, FS:])
    shared_part = matmul(shared_hidden, shared_out)
    pair_expert, slot_index = slot_plan(route_rows, prio_row)
    kept_mask = (slot_index < CAP).astype(jnp.float32)
    slot_clip = jnp.minimum(slot_index, CAP - 1)
    owner_token = jnp.arange(row_count * TOP, dtype=jnp.int32) // TOP
    buffer = jnp.zeros((EXPERTS, CAP, D), jnp.float32).at[pair_expert, slot_clip].add(normed_two[owner_token] * kept_mask[:, None])
    buffer = low_back(buffer)
    expert_pre = low_back(jnp.einsum('ecd,edf->ecf', buffer, expert_in, precision=highest))
    expert_hidden = low(jax.nn.silu(expert_pre[..., :FF]) * expert_pre[..., FF:])
    expert_result = low(low_back(jnp.einsum('ecf,efd->ecd', expert_hidden, expert_out, precision=highest)))
    pair_result = expert_result[pair_expert, slot_clip] * kept_mask[:, None]
    pair_gate = jnp.take_along_axis(gate_probs, route_rows, axis=1).reshape(-1)
    routed = lax.optimization_barrier(jnp.sum((pair_gate[:, None] * pair_result).reshape(row_count, TOP, D), axis=1))
    return residual + shared_part + routed

def reference(layer_input, routes, priority, cont_ids, cotangent, norm1_gain, qkv_weight, out_weight, norm2_gain, router_weight, shared_in, shared_out, expert_in, expert_out):
    params = tuple((member_array.astype(jnp.float32) for member_array in (norm1_gain, qkv_weight, out_weight, norm2_gain, router_weight, shared_in, shared_out, expert_in, expert_out)))
    groups = layer_input.shape[0] // TOK_DEV
    inputs = layer_input.astype(jnp.float32).reshape(groups, TOK_DEV, D)
    route_groups = routes.reshape(groups, TOK_DEV, TOP)

    def whole_layer(params, inputs):

        def one_group(pieces):
            tokens, route_rows, prio_row, cont_row = pieces
            return group_forward(params, tokens, route_rows, prio_row, cont_row)
        return lax.map(jax.checkpoint(one_group), (inputs, route_groups, priority, cont_ids))
    result, pullback = jax.vjp(whole_layer, params, inputs)
    param_grads, input_grad = pullback(cotangent.astype(jnp.float32).reshape(groups, TOK_DEV, D))
    return (result.reshape(-1, D).astype(jnp.bfloat16), input_grad.reshape(-1, D), param_grads[0], param_grads[1], param_grads[2], param_grads[3], param_grads[4], param_grads[5], param_grads[6], param_grads[7], param_grads[8])
```

```python
from functools import partial

import jax
import jax.numpy as jnp
from jax import lax
from jax.sharding import Mesh
from jax.sharding import PartitionSpec as P

D = 768
HEADS = 12
HEAD = 64
EXPERTS = 16
FF = 2048
TOP = 2
FS = 2048
CONTS = 4
TOK_DEV = 256
PROMPT = 128
CAP = 40


epsilon = 1e-06
rope_base = 10000.0
highest = lax.Precision.HIGHEST
bfloat = jnp.bfloat16
single = jnp.float32


def layout(cont_row):
    labels = jnp.arange(CONTS, dtype=jnp.int32)
    member = cont_row[:, None] == labels[None, :]
    lengths = jnp.sum(member.astype(jnp.int32), axis=0)
    starts = jnp.cumsum(lengths) - lengths
    begins = jnp.sum(jnp.where(member, starts[None, :], 0), axis=1)
    offsets = jnp.arange(cont_row.shape[0], dtype=jnp.int32) - begins
    position = jnp.concatenate([jnp.arange(PROMPT, dtype=jnp.int32), PROMPT + offsets])
    segment = jnp.concatenate([jnp.full((PROMPT,), -1, jnp.int32), cont_row])
    rows_at = jnp.arange(TOK_DEV, dtype=jnp.int32)
    visible = (rows_at[None, :] <= rows_at[:, None]) & (segment[None, :] == segment[:, None]) | (
        rows_at[None, :] < PROMPT
    ) & (rows_at[:, None] >= PROMPT)
    half_dim = HEAD // 2
    frequency = rope_base ** (-(jnp.arange(half_dim, dtype=single) * 2.0) / HEAD)
    angles = position.astype(single)[:, None] * frequency[None, :]
    cosine = jnp.concatenate([jnp.cos(angles), jnp.cos(angles)], axis=1)
    sine_table = jnp.concatenate([jnp.sin(angles), jnp.sin(angles)], axis=1)
    return (visible, cosine, sine_table)


def rotate(values, cosine, sine_table):
    half_dim = HEAD // 2
    turned = jnp.concatenate([-values[..., half_dim:], values[..., :half_dim]], axis=-1)
    return values * cosine[:, None, :] + turned * sine_table[:, None, :]


def unrotate(gradient, cosine, sine_table):
    half_dim = HEAD // 2
    turned = jnp.concatenate([gradient[..., half_dim:], -gradient[..., :half_dim]], axis=-1)
    return gradient * cosine[:, None, :] + turned * sine_table[:, None, :]


def swish(gate_part):
    return gate_part * jax.nn.sigmoid(gate_part)


def swish_slope(gate_part):
    sigmoid_value = jax.nn.sigmoid(gate_part)
    return sigmoid_value * (1.0 + gate_part * (1.0 - sigmoid_value))


def slot_plan(route_rows, prio_row):
    expert_of = route_rows.reshape(-1)
    ahead = (expert_of[:, None] == expert_of[None, :]) & (prio_row[None, :] < prio_row[:, None])
    return jnp.sum(ahead.astype(jnp.int32), axis=1).reshape(route_rows.shape)


def flip(value):
    return lax.ppermute(value, "core", [(0, 1), (1, 0)])


def halves(wide, blocks):
    size = wide.shape[-1] // blocks
    half = size // 2
    return tuple(
        jnp.concatenate(
            [wide[..., b * size + c * half : b * size + (c + 1) * half] for b in range(blocks)],
            axis=-1,
        )
        for c in range(2)
    )


def rejoin(first, second, blocks):
    half = first.shape[-1] // blocks
    pieces = []
    for b in range(blocks):
        pieces += [first[..., b * half : (b + 1) * half], second[..., b * half : (b + 1) * half]]
    return jnp.concatenate(pieces, axis=-1)


def pair_forward(visible, pieces):
    query_pair, key_pair, value_pair = pieces
    scores = jnp.einsum("qhd,khd->hqk", query_pair, key_pair, preferred_element_type=single) * 0.125
    scores = jnp.where(visible[None], scores, -1e30)
    top_score = jnp.max(scores, axis=-1, keepdims=True)
    weights = jnp.exp(scores - top_score)
    totals = jnp.sum(weights, axis=-1, keepdims=True)
    attention = (weights / totals).astype(bfloat)
    context = jnp.einsum("hqk,khd->qhd", attention, value_pair, preferred_element_type=single)
    return (context.astype(bfloat), (top_score + jnp.log(totals))[..., 0])


def pair_backward(visible, pieces):
    query_pair, key_pair, value_pair, log_total, grad_context = pieces
    scores = jnp.einsum("qhd,khd->hqk", query_pair, key_pair, preferred_element_type=single) * 0.125
    scores = jnp.where(visible[None], scores, -1e30)
    attention = jnp.exp(scores - log_total[..., None])
    attention_low = attention.astype(bfloat)
    grad_value = jnp.einsum(
        "hqk,qhd->khd", attention_low, grad_context, preferred_element_type=single
    )
    grad_attention = jnp.einsum(
        "qhd,khd->hqk", grad_context, value_pair, preferred_element_type=single
    )
    grad_scores = (
        attention * (grad_attention - jnp.sum(attention * grad_attention, axis=-1, keepdims=True))
    ).astype(bfloat)
    grad_query = (
        jnp.einsum("hqk,khd->qhd", grad_scores, key_pair, preferred_element_type=single) * 0.125
    )
    grad_key = (
        jnp.einsum("hqk,qhd->khd", grad_scores, query_pair, preferred_element_type=single) * 0.125
    )
    return (grad_query, grad_key, grad_value)


CHIPS = ("r", "j", "x")
DEVICES = ("r", "j", "x", "core")
PEERS = ("x", "core")
ROWS = ("r", "j")
OWNERS = ("x", "core", "j")


def swiglu(pre, width):
    return (swish(pre[:, :width]) * pre[:, width:]).astype(bfloat)


def swiglu_back(grad, pre, width):
    gate, up = pre[:, :width], pre[:, width:]
    return jnp.concatenate([grad * up * swish_slope(gate), grad * swish(gate)], axis=-1).astype(
        bfloat
    )


def dot(left, right, left_axis=1, right_axis=0):
    return lax.dot_general(
        left, right, (((left_axis,), (right_axis,)), ((), ())), preferred_element_type=single
    )


def local(
    layer_input,
    routes,
    priority,
    cont_ids,
    cotangent,
    norm1_gain,
    qkv_weight,
    out_weight,
    norm2_gain,
    router_weight,
    shared_in,
    shared_out,
    expert_in,
    expert_out,
):
    row_count = layer_input.shape[0]
    spans_x = lax.axis_size("x")
    owners = lax.axis_size("j")
    copies = lax.axis_size("r")
    shards = copies * owners
    core = lax.axis_index("core")
    x_at = lax.axis_index("x")
    first_core = core == 0
    half_ff = FF // 2
    half_fs = FS // 2
    shard_rows = D // shards
    block = FF // shards

    def mine_of(pair):
        return jnp.where(first_core, pair[0], pair[1])

    def other_of(pair):
        return jnp.where(first_core, pair[1], pair[0])

    def part(rows, index, count):
        size = rows.shape[0] // count
        return lax.dynamic_slice_in_dim(rows, index * size, size, 0)

    packed = jnp.concatenate(
        [
            qkv_weight,
            norm1_gain[:, None],
            norm2_gain[:, None],
            router_weight,
            jnp.zeros((shard_rows, 110), bfloat),
        ],
        axis=1,
    )
    peer = x_at * 2 + core
    packed_full = lax.all_gather(part(packed, peer, spans_x * 2), DEVICES, axis=0, tiled=True)
    outw_full = lax.all_gather(part(out_weight, peer, spans_x * 2), DEVICES, axis=0, tiled=True)
    shared_wide = lax.all_gather(
        mine_of(halves(part(shared_in, x_at, spans_x), 2 * shards)), CHIPS, axis=0, tiled=True
    )
    shared_down = lax.all_gather(
        part(part(shared_out, core, 2), x_at, spans_x), CHIPS, axis=0, tiled=True
    )
    qkv_full = packed_full[:, : 3 * D]
    gain_one = packed_full[:, 3 * D].astype(single)
    gain_two = packed_full[:, 3 * D + 1].astype(single)
    router_full = packed_full[:, 3 * D + 2 : 3 * D + 2 + EXPERTS]

    in_pair = halves(expert_in, 2 * shards)
    out_pair = (expert_out[:, : block // 2], expert_out[:, block // 2 :])

    def to_owner(pair):
        mine, other = mine_of(pair), flip(other_of(pair))
        whole = jnp.where(
            first_core, jnp.concatenate([mine, other]), jnp.concatenate([other, mine])
        )
        whole = jnp.tile(whole, (copies, 1, 1))
        return lax.all_to_all(whole, ROWS, split_axis=0, concat_axis=0, tiled=True)

    expert_wide = to_owner(in_pair).reshape(D, 2 * half_ff)
    expert_down = to_owner(out_pair).reshape(half_ff, D)

    visible, cosine, sine_table = layout(cont_ids[0])

    def by_pairs(stacked):
        return jnp.moveaxis(stacked.reshape(row_count, HEADS // 2, 2, HEAD), 1, 0)

    def from_pairs(stacked):
        return jnp.moveaxis(stacked, 0, 1).reshape(row_count, D)

    inputs = layer_input.astype(single)
    scale_one = lax.rsqrt(jnp.mean(inputs * inputs, axis=-1, keepdims=True) + epsilon)
    normal_one = inputs * scale_one
    hidden_one = (normal_one * gain_one).astype(bfloat)
    projected = dot(hidden_one, qkv_full)
    queries = rotate(projected[:, :D].reshape(row_count, HEADS, HEAD), cosine, sine_table).astype(
        bfloat
    )
    key_heads = rotate(
        projected[:, D : 2 * D].reshape(row_count, HEADS, HEAD), cosine, sine_table
    ).astype(bfloat)
    values = projected[:, 2 * D :].astype(bfloat)
    context_pairs, log_totals = lax.map(
        partial(pair_forward, visible), (by_pairs(queries), by_pairs(key_heads), by_pairs(values))
    )
    context = from_pairs(context_pairs)
    residual = inputs + dot(context, outw_full)
    scale_two = lax.rsqrt(jnp.mean(residual * residual, axis=-1, keepdims=True) + epsilon)
    normal_two = residual * scale_two
    hidden_two = (normal_two * gain_two).astype(bfloat)
    gate_probs = jax.nn.softmax(dot(hidden_two, router_full), axis=-1)

    slot_index = slot_plan(routes, priority[0])
    spot = ((routes // owners) * 2 * owners + routes % owners) * CAP + slot_index
    spot = jnp.where(slot_index < CAP, spot, -1)
    exchange = spans_x * 2 * owners * CAP
    places = jnp.arange(exchange, dtype=jnp.int32)
    shift = owners * CAP
    takes = [
        (places[:, None] == spot[None, :, k]) for k in range(TOP)
    ]
    pair_gate = jnp.take_along_axis(gate_probs, routes, axis=1)
    token_pick = (takes[0] | takes[1]).astype(bfloat).reshape(spans_x, 2, shift, row_count)[:, 0]
    token_pick = token_pick.reshape(spans_x * shift, row_count)
    slot_gate = sum(
        jnp.sum(
            jnp.where(takes[k].reshape(spans_x, 2, shift, row_count)[:, 0], pair_gate[:, k], 0.0),
            axis=-1,
        )
        for k in range(TOP)
    ).reshape(spans_x * shift, 1)
    slot_hidden = dot(token_pick, hidden_two).astype(bfloat)
    slot_grad = (slot_gate * dot(token_pick, cotangent)).astype(bfloat)
    outgoing = jnp.stack(
        [slot_hidden.reshape(spans_x, shift, D), slot_grad.reshape(spans_x, shift, D)], axis=1
    ).reshape(exchange, D)
    arrived = lax.all_to_all(outgoing, OWNERS, split_axis=0, concat_axis=0, tiled=True)

    pair_hidden = jnp.concatenate([hidden_two, flip(hidden_two)])
    pair_cotangent = jnp.concatenate([cotangent, flip(cotangent)])
    shared_pre = dot(pair_hidden, shared_wide)
    shared_hidden = swiglu(shared_pre, half_fs)
    shared_part = dot(shared_hidden, shared_down)
    shared_part = shared_part[:row_count] + flip(shared_part[row_count:].astype(bfloat)).astype(
        single
    )
    shared_out_grad = dot(shared_hidden, pair_cotangent, 0, 0).astype(bfloat)
    grad_shared_pre = swiglu_back(dot(pair_cotangent, shared_down, 1, 1), shared_pre, half_fs)
    shared_in_grad = dot(pair_hidden, grad_shared_pre, 0, 0).astype(bfloat)
    grad_shared = dot(grad_shared_pre, shared_wide, 1, 1)
    grad_shared = grad_shared[:row_count] + flip(grad_shared[row_count:].astype(bfloat)).astype(
        single
    )
    shared_in_sum = lax.psum_scatter(shared_in_grad, CHIPS, scatter_dimension=0, tiled=True)
    shared_out_sum = lax.psum_scatter(shared_out_grad, CHIPS, scatter_dimension=0, tiled=True)
    shared_in_sum = lax.all_gather(shared_in_sum, PEERS, axis=0, tiled=False)
    shared_in_sum = shared_in_sum.reshape(spans_x, 2, shard_rows // spans_x, FS)
    shared_in_sum = rejoin(
        shared_in_sum[:, 0].reshape(shard_rows, FS),
        shared_in_sum[:, 1].reshape(shard_rows, FS),
        2 * shards,
    ).astype(single)
    shared_out_sum = lax.all_gather(shared_out_sum, PEERS, axis=0, tiled=False)
    shared_out_sum = (
        jnp.moveaxis(shared_out_sum.reshape(spans_x, 2, -1, D), 1, 0).reshape(FS // shards, D)
    ).astype(single)

    crossed = flip(arrived)
    buffer = jnp.where(first_core, arrived, crossed)
    grad_buffer = jnp.where(first_core, crossed, arrived)
    expert_pre = dot(buffer, expert_wide)
    expert_hidden = swiglu(expert_pre, half_ff)
    expert_result = dot(expert_hidden, expert_down)
    grad_expert_pre = swiglu_back(dot(grad_buffer, expert_down, 1, 1), expert_pre, half_ff)
    grad_rows = dot(grad_expert_pre, expert_wide, 1, 1)
    kept = jnp.where(first_core, expert_result, grad_rows)
    given = jnp.where(first_core, grad_rows, expert_result).astype(bfloat)
    finished = (kept + flip(given).astype(single)).astype(bfloat)
    returned = lax.all_to_all(finished, OWNERS, split_axis=0, concat_axis=0, tiled=True)

    expert_out_grad = dot(expert_hidden, grad_buffer, 0, 0).astype(bfloat)
    expert_in_grad = dot(buffer, grad_expert_pre, 0, 0).astype(bfloat)

    def to_shards(grads):
        spread = lax.all_to_all(grads, ROWS, split_axis=0, concat_axis=0, tiled=True)
        spread = spread.reshape((copies, owners) + spread.shape[1:])
        if copies > 1:
            spread = jnp.sum(spread.astype(single), axis=0).astype(bfloat)
        else:
            spread = spread[0]
        low, high = spread[: owners // 2], spread[owners // 2 :]
        mine = jnp.where(first_core, low, high)
        other = flip(jnp.where(first_core, high, low))
        return (jnp.where(first_core, mine, other), jnp.where(first_core, other, mine))

    expert_in_sum = rejoin(
        *to_shards(expert_in_grad.reshape(shards, shard_rows, 2 * half_ff)), 2 * shards
    ).astype(single)
    expert_out_sum = jnp.concatenate(
        to_shards(expert_out_grad.reshape(shards, block // 2, D)), axis=1
    ).astype(single)

    result_picks = [(spot[:, k, None] == places[None, :]).astype(bfloat) for k in range(TOP)]
    pair_results = [dot(pick, returned) for pick in result_picks]
    routed = sum(pair_gate[:, k, None] * pair_results[k] for k in range(TOP))
    output = (residual + shared_part + routed).astype(bfloat)
    grad_output = cotangent.astype(single)
    expert_ids = jnp.arange(EXPERTS, dtype=jnp.int32)
    grad_gates = sum(
        jnp.where(
            routes[:, k, None] == expert_ids[None, :],
            jnp.sum(grad_output * pair_results[k], axis=-1, keepdims=True),
            0.0,
        )
        for k in range(TOP)
    )
    grad_logits = gate_probs * (
        grad_gates - jnp.sum(gate_probs * grad_gates, axis=-1, keepdims=True)
    )
    router_grad = jnp.einsum(
        "td,te->de", hidden_two.astype(single), grad_logits, precision=highest
    )
    back_spot = jnp.where(spot >= 0, spot + shift, -1)
    back_pick = (
        (back_spot[:, 0, None] == places[None, :]) | (back_spot[:, 1, None] == places[None, :])
    ).astype(bfloat)
    grad_hidden_two = dot(back_pick, returned) + grad_shared
    grad_hidden_two = grad_hidden_two + jnp.einsum(
        "te,de->td", grad_logits, router_full.astype(single), precision=highest
    )
    norm2_grad = jnp.sum(grad_hidden_two * normal_two, axis=0)
    grad_normal_two = grad_hidden_two * gain_two
    grad_residual = grad_output + scale_two * (
        grad_normal_two
        - normal_two * jnp.mean(grad_normal_two * normal_two, axis=-1, keepdims=True)
    )
    grad_residual_low = grad_residual.astype(bfloat)
    out_weight_grad = dot(context, grad_residual_low, 0, 0).astype(bfloat)
    grad_context = dot(grad_residual_low, outw_full, 1, 1).astype(bfloat)
    grad_query_pairs, grad_key_pairs, grad_value_pairs = lax.map(
        partial(pair_backward, visible),
        (
            by_pairs(queries),
            by_pairs(key_heads),
            by_pairs(values),
            log_totals,
            by_pairs(grad_context),
        ),
    )
    grad_query = unrotate(
        from_pairs(grad_query_pairs).reshape(row_count, HEADS, HEAD), cosine, sine_table
    ).reshape(row_count, D)
    grad_key = unrotate(
        from_pairs(grad_key_pairs).reshape(row_count, HEADS, HEAD), cosine, sine_table
    ).reshape(row_count, D)
    grad_projected = jnp.concatenate(
        [grad_query, grad_key, from_pairs(grad_value_pairs)], axis=1
    ).astype(bfloat)
    qkv_grad = dot(hidden_one, grad_projected, 0, 0).astype(bfloat)
    grad_hidden_one = dot(grad_projected, qkv_full, 1, 1)
    norm1_grad = jnp.sum(grad_hidden_one * normal_one, axis=0)
    grad_normal_one = grad_hidden_one * gain_one
    input_grad = grad_residual + scale_one * (
        grad_normal_one
        - normal_one * jnp.mean(grad_normal_one * normal_one, axis=-1, keepdims=True)
    )

    def reduce_rows(grads):
        summed = lax.psum_scatter(grads, DEVICES, scatter_dimension=0, tiled=True)
        return lax.all_gather(summed, PEERS, axis=0, tiled=True).astype(single)

    outw_sum = reduce_rows(out_weight_grad)
    packed_sum = reduce_rows(
        jnp.concatenate(
            [
                qkv_grad,
                norm1_grad[:, None].astype(bfloat),
                norm2_grad[:, None].astype(bfloat),
                router_grad.astype(bfloat),
                jnp.zeros((D, 110), bfloat),
            ],
            axis=1,
        )
    )
    return (
        output,
        input_grad,
        packed_sum[:, 3 * D],
        packed_sum[:, : 3 * D],
        outw_sum,
        packed_sum[:, 3 * D + 1],
        packed_sum[:, 3 * D + 2 : 3 * D + 2 + EXPERTS],
        shared_in_sum,
        shared_out_sum,
        expert_in_sum,
        expert_out_sum,
    )


def solution(mesh):
    spans_x = mesh.shape["expert"] // 2
    owners = EXPERTS // spans_x
    view = Mesh(
        mesh.devices.reshape(spans_x, 2, mesh.shape["dp"] // owners, owners),
        ("x", "core", "r", "j"),
    )
    tokens = P(("x", "core", "r", "j"), None)
    vector = P(("r", "j"))
    rows = P(("r", "j"), None)
    experts = P(("x", "core"), ("r", "j"), None)
    return jax.shard_map(
        local,
        mesh=view,
        in_specs=(
            (tokens,) * 5
            + (vector, rows, rows, vector, rows, rows, rows, experts, experts)
        ),
        out_specs=(tokens, tokens, vector, rows, rows, vector, rows, rows, rows, experts, experts),
        check_vma=False,
    )
```
